32 devices in a mesh: grp: 2 (over x), tile: 16 (over z, y, core).
Axes of the slice: x: 2, y: 2, z: 4, core: 2. Of those that a mesh axis runs over, the one named last changes fastest.
Arguments:
- features: bfloat16 [384, 64, 2048], P('tile', 'grp'), may hold values from -6 to 6
- occupancy: int32 [192, 2, 16], P('tile', 'grp'), may hold values 0 or 1
- link_weights: int32 [4, 384, 64], P(None, 'tile', 'grp'), may hold values from 0 to 3
- basis_cols: bfloat16 [2048, 256], replicated, may hold values from -0.125 to 0.125
Outputs:
- product: float32 [2048, 256], P('tile')
The draws below stay inside these ranges and needn't reach their ends.
All inputs are finite; a program needn't handle non-finite values. No bound on the sum of `occupancy` on one device may be relied on, other than what follows from the above.
Results may differ from the reference program's by a relative error of at most 0.004.
Values may be sent and summed in bfloat16 or wider, within the bound.
No kernel may reach another device: no remote copies, remote signals or barrier semaphores. Data moves between devices by JAX's collectives and lax.ppermute only.
A program may use at most 64 MiB of HBM per device.

```python
import math
import jax
import jax.numpy as jnp
from jax import lax

WORDS = 2048
RANK = 256
WB = 128
NLAT = 384
NLON = 64
N_GRP = 2


def place_ends(result, key, least, largest):
    longest = result.shape.index(max(result.shape))
    spots = []
    for shift in (0, 1):
        where = [jax.random.randint(jax.random.fold_in(key, axis), (), 0, length) for axis, length in enumerate(result.shape)]
        where[longest] = (where[longest] + shift) % result.shape[longest]
        spots.append(tuple(where))
    return result.at[spots[0]].set(least).at[spots[1]].set(largest)


def strengthened(values, own_key, source, target, shards_of, factor):
    owner, partner = [(jnp.arange(values.shape[dim]) // (values.shape[dim] // shards_of)).reshape([-1 if axis == dim else 1 for axis in range(values.ndim)]) for dim in (source, target)]
    chosen = jax.random.permutation(own_key, shards_of)[partner]
    strong = (owner == chosen) | (owner == (partner + shards_of // 2) % shards_of)
    return jnp.where(strong, factor * values, values)


def steps_of(key, shape, pieces, smallest, high):
    loudness, own = 1.0, jax.random.fold_in(key, 6)
    for position, parts in pieces:
        draws = jnp.exp(jax.random.uniform(jax.random.fold_in(own, position), (parts,), jnp.float32, smallest / len(pieces), high / len(pieces)))
        loudness = loudness * jnp.repeat(draws, shape[position] // parts).reshape([-1 if axis == position else 1 for axis in range(len(shape))])
    return loudness


def centred(key, dims, spread, bound, split=(), kind=jnp.bfloat16):
    result = jax.random.normal(key, dims, jnp.float32) * spread
    if len(split) > 0:
        result = steps_of(key, dims, split, -0.22, 0.18) * result
    return jnp.clip(result, min=-bound, max=bound).astype(kind)


def heavy_noise(rng, extent, spread, limit, pieces, heavy, kind=jnp.bfloat16):
    values = spread * jax.random.normal(rng, extent, jnp.float32)
    if pieces:
        values = values * steps_of(rng, extent, pieces, -0.22, 0.18)
    return jnp.clip(strengthened(values, jax.random.fold_in(rng, 3), *heavy), -limit, limit).astype(kind)


def setup_inputs(seed: int = 0) -> dict:
    key_of = jax.random.split(jax.random.key(seed), 5)
    return {
        "features": heavy_noise(key_of[0], (NLAT, NLON, WORDS), 1.0, 6.0, ((0, 16), (1, 2)), (0, 2, 16, 2.0)),
        "occupancy": place_ends((jax.random.randint(key_of[1], (NLAT // 2, N_GRP, WORDS // WB), 0, 5) < 3).astype(jnp.int32), jax.random.fold_in(key_of[1], 1), 0, 1),
        "link_weights": place_ends(jax.random.randint(key_of[2], (4, NLAT, NLON), 0, 4), jax.random.fold_in(key_of[2], 1), 0, 3).astype(jnp.int32),
        "basis_cols": centred(key_of[3], (WORDS, RANK), WORDS ** -0.5, 0.125),
    }


def apply_mask(feat_rows, mask_rows):
    lat_rows, lon_cols, word_count = feat_rows.shape
    groups = mask_rows.shape[1]
    word_blocks = mask_rows.shape[2]
    shaped = feat_rows.reshape(lat_rows // 2, 2, groups, lon_cols // groups, word_blocks, word_count // word_blocks)
    gate = mask_rows.astype(jnp.bfloat16)[:, None, :, None, :, None]
    return (shaped * gate).reshape(lat_rows * lon_cols, word_count)

def spatial_average(padded, link_weights):
    weights = link_weights.astype(jnp.float32)
    north_side = padded[:-2, 1:-1].astype(jnp.float32)
    south_side = padded[2:, 1:-1].astype(jnp.float32)
    west_side = padded[1:-1, :-2].astype(jnp.float32)
    east_side = padded[1:-1, 2:].astype(jnp.float32)
    weighted = weights[0][:, :, None] * north_side + weights[1][:, :, None] * south_side
    weighted = weighted + weights[2][:, :, None] * west_side + weights[3][:, :, None] * east_side
    weight_total = jnp.maximum(lax.optimization_barrier(jnp.sum(weights, axis=0)), 1.0)
    return (weighted / weight_total[:, :, None]).astype(jnp.bfloat16)

def reference(features, occupancy, link_weights, basis_cols):
    feat_blocks = features.reshape(NLAT // 2, 2, NLON, WORDS)

    def project(inputs):
        feat_rows, mask_rows = inputs
        masked = apply_mask(feat_rows, mask_rows[None])
        return jnp.dot(masked, basis_cols, preferred_element_type=jnp.float32).astype(jnp.bfloat16)
    projected = lax.map(project, (feat_blocks, occupancy)).reshape(NLAT, NLON, RANK)
    padded = jnp.pad(projected, ((1, 1), (1, 1), (0, 0)))
    smooth = spatial_average(padded, link_weights).reshape(NLAT // 2, 2 * NLON, RANK)

    def accumulate(running, inputs):
        feat_rows, mask_rows, smooth_rows = inputs
        masked = apply_mask(feat_rows, mask_rows[None])
        term = lax.dot_general(masked, smooth_rows, (((0,), (0,)), ((), ())), preferred_element_type=jnp.float32)
        return (running + term, None)
    running, _ = lax.scan(accumulate, jnp.zeros((WORDS, RANK), jnp.float32), (feat_blocks, occupancy, smooth))
    return running * (1.0 / math.sqrt(NLAT * NLON))
```

```python
import functools
import math

import jax
import jax.numpy as jnp
from jax import lax
from jax.experimental import pallas as pl
from jax.experimental.pallas import tpu as pltpu
from jax.sharding import PartitionSpec as P

F32 = jnp.float32
BF16 = jnp.bfloat16
AXES = ("grp", "tile")
IN_HBM = pl.BlockSpec(memory_space=pltpu.HBM)
IN_VMEM = pl.BlockSpec(memory_space=pltpu.VMEM)
KERNEL_VMEM = 24 << 20
WORD_CHUNK = 512


def project_kernel(occ_hbm, feat_hbm, basis_hbm, masked, proj, *rest):
    *edges, basis, total, occ, sems = rest
    row_a, row_b = edges[:2]
    lat, lon, words = masked.shape
    blocks = occ.shape[2]
    block = words // blocks
    chunk = min(WORD_CHUNK, words)
    count = words // chunk
    occ_copy = pltpu.make_async_copy(occ_hbm, occ, sems.at[2 * count])
    occ_copy.start()
    copies = []
    for k in range(count):
        part = pl.ds(k * chunk, chunk)
        basis_copy = pltpu.make_async_copy(basis_hbm.at[part], basis.at[part], sems.at[count + k])
        feat_copy = pltpu.make_async_copy(feat_hbm.at[:, :, part], masked.at[:, :, part], sems.at[k])
        basis_copy.start()
        feat_copy.start()
        copies.append((basis_copy, feat_copy))
    occ_copy.wait()
    for k in range(count):
        copies[k][0].wait()
        copies[k][1].wait()
        for i in range(lat // 2):
            for b in range(k * chunk // block, (k + 1) * chunk // block):
                gate = occ[i, 0, b].astype(F32).astype(BF16)
                spot = (pl.ds(2 * i, 2), slice(None), pl.ds(b * block, block))
                masked[spot] = masked[spot] * gate
        part = pl.ds(k * chunk, chunk)
        term = jnp.dot(
            masked[:, :, part].reshape(lat * lon, chunk), basis[part, :], preferred_element_type=F32
        )
        if k:
            term = total[...] + term
        if k < count - 1:
            total[...] = term
    rounded = term.astype(BF16)
    proj[...] = rounded.reshape(proj.shape)
    north, south = rounded[:lon], rounded[-lon:]
    even = lax.rem(lax.axis_index("tile"), 2) == 0
    row_a[...] = jnp.where(even, south, north)
    row_b[...] = jnp.where(even, north, south)
    grid = term.reshape(lat, lon, -1)
    west, east = grid[:, 0, :], grid[:, lon - 1, :]
    even = lax.rem(lax.axis_index("grp"), 2) == 0
    edges[2][...] = jnp.where(even, east, west).astype(BF16)
    if len(edges) > 3:
        edges[3][...] = jnp.where(even, west, east).astype(BF16)


def project(occupancy, features, basis_cols, columns):
    lat, lon, words = features.shape
    rank = basis_cols.shape[1]
    count = words // min(WORD_CHUNK, words)
    operands = [pltpu.with_memory_space_constraint(v, pltpu.HBM) for v in (occupancy, features, basis_cols)]
    return pl.pallas_call(
        project_kernel,
        out_shape=(
            pltpu.VMEM((lat, lon, words), BF16),
            pltpu.VMEM((lat, lon, rank), BF16),
            pltpu.VMEM((lon, rank), BF16),
            pltpu.VMEM((lon, rank), BF16),
        ) + (pltpu.VMEM((lat, rank), BF16),) * columns,
        in_specs=[IN_HBM] * 3,
        out_specs=(IN_VMEM,) * (4 + columns),
        scratch_shapes=[
            pltpu.VMEM(basis_cols.shape, BF16),
            pltpu.VMEM((lat * lon, rank), F32),
            pltpu.SMEM(occupancy.shape, jnp.int32),
            pltpu.SemaphoreType.DMA((2 * count + 1,)),
        ],
        compiler_params=pltpu.CompilerParams(vmem_limit_bytes=KERNEL_VMEM),
        cost_estimate=pl.CostEstimate(
            flops=2 * lat * lon * words * rank, bytes_accessed=2 * lat * lon * words, transcendentals=0
        ),
    )(*operands)


def smooth_rows(proj, north, south, west, east, links, smooth):
    lat, lon, rank = proj.shape
    weights = links[...].astype(F32)
    weights = weights / jnp.maximum(jnp.sum(weights, axis=0), 1.0)
    columns = [jnp.transpose(weights[k]) for k in range(4)]
    place = lax.broadcasted_iota(jnp.int32, (lon, rank), 0)
    for i in range(lat):
        row = proj[i].astype(F32)
        above = proj[i - 1].astype(F32) if i else north
        below = proj[i + 1].astype(F32) if i < lat - 1 else south
        left = jnp.where(place == 0, west[i:i + 1, :], pltpu.roll(row, 1, 0))
        right = jnp.where(place == lon - 1, east[i:i + 1, :], pltpu.roll(row, lon - 1, 0))
        link = [jnp.broadcast_to(columns[k][:, i:i + 1], (lon, rank)) for k in range(4)]
        value = link[0] * above + link[1] * below + link[2] * left + link[3] * right
        smooth[pl.ds(i * lon, lon), :] = value.astype(BF16)


def partial_kernel(orders, masked, proj, halo_row_a, halo_row_b, *rest):
    *halo_cols, links, send, keep, smooth = rest
    lat, lon, words = masked.shape
    rank = proj.shape[2]
    pairs, share = send.shape[:2]
    row_a, row_b = halo_row_a[...].astype(F32), halo_row_b[...].astype(F32)
    odd = lax.rem(lax.axis_index("tile"), 2)
    north = jnp.where(odd == 0, row_b, row_a)
    south = jnp.where(odd == 0, row_a, row_b)
    col_a = halo_cols[0][...].astype(F32)
    col_b = halo_cols[1][...].astype(F32) if len(halo_cols) > 1 else jnp.zeros_like(col_a)
    even = lax.rem(lax.axis_index("grp"), 2) == 0
    west = jnp.where(even, col_b, col_a)
    east = jnp.where(even, col_a, col_b)
    smooth_rows(proj, north, south, west, east, links, smooth)
    values = smooth[...]
    step = 256
    for first in range(0, words, step):
        part = masked[:, :, pl.ds(first, step)].reshape(lat * lon, step)
        term = lax.dot_general(part, values, (((0,), (0,)), ((), ())), preferred_element_type=F32)
        for at in range(0, step, 2 * share):
            pair = (first + at) // (2 * share)
            here = jnp.where(odd == 0, orders[0][pair], orders[1][pair])
            there = jnp.where(odd == 0, orders[1][pair], orders[0][pair])
            low, high = term[at:at + share], term[at + share:at + 2 * share]
            send[there] = jnp.where(odd == 0, high, low).astype(BF16)
            keep[here] = jnp.where(odd == 0, low, high)


def partial_product(orders, share, masked, proj, rows, cols, link_weights):
    lat, lon, words = masked.shape
    rank = proj.shape[2]
    pairs = words // share // 2
    return pl.pallas_call(
        functools.partial(partial_kernel, orders),
        out_shape=(pltpu.VMEM((pairs, share, rank), BF16), pltpu.VMEM((pairs, share, rank), F32)),
        in_specs=[IN_VMEM] * (5 + len(cols)),
        out_specs=(IN_VMEM,) * 2,
        scratch_shapes=[pltpu.VMEM((lat * lon, rank), BF16)],
        compiler_params=pltpu.CompilerParams(vmem_limit_bytes=KERNEL_VMEM),
        cost_estimate=pl.CostEstimate(
            flops=2 * lat * lon * words * rank, bytes_accessed=2 * lat * lon * words, transcendentals=0
        ),
    )(masked, proj, *rows, *cols, link_weights)


def bit_orders(bits):
    plain = list(range(1, bits))
    turned = plain[1::-1] + plain[2:]
    return plain, turned


def block_places(order):
    steps = len(order)
    places = []
    for pair in range(1 << steps):
        tile = pair << 1
        places.append(sum(((tile >> bit) & 1) << (steps - 1 - j) for j, bit in enumerate(order)))
    return tuple(places)


def per_device(groups, tiles, features, occupancy, link_weights, basis_cols):
    lat, lon, words = features.shape
    share = words // tiles
    bits = tiles.bit_length() - 1
    orders = bit_orders(bits)
    tile = lax.axis_index("tile")
    core = lax.rem(tile, 2)

    def exchange(values, partner):
        pairs = []
        for g in range(groups):
            for t in range(tiles):
                to_g, to_t = partner(g, t)
                if 0 <= to_g < groups and 0 <= to_t < tiles:
                    pairs.append((g * tiles + t, to_g * tiles + to_t))
        return lax.ppermute(values, AXES, pairs)

    masked, proj, row_a, row_b, *cols = project(occupancy, features, basis_cols, 1 if groups <= 2 else 2)
    halo_row_b = exchange(row_b, lambda g, t: (g, t - 1 + 2 * (t % 2)))
    halo_cols = [exchange(cols[0], lambda g, t: (g + 1 - 2 * (g % 2), t))]
    if groups > 2:
        halo_cols.append(exchange(cols[1], lambda g, t: (g - 1 + 2 * (g % 2), t)))
    halo_row_a = exchange(row_a, lambda g, t: (g, t ^ 1))
    send, held = partial_product(
        tuple(block_places(order) for order in orders),
        share, masked, proj, (halo_row_a, halo_row_b), halo_cols, link_weights,
    )
    got = exchange(send, lambda g, t: (g, t ^ 1))
    pick = functools.partial(lax.dynamic_index_in_dim, axis=0, keepdims=False)
    for j in range(bits - 1):
        bit = jnp.where(core == 0, orders[0][j], orders[1][j])
        mine = lax.rem(lax.shift_right_logical(tile, bit), 2)
        halves = (2, held.shape[0] // 2) + held.shape[1:]
        held, got = held.reshape(halves), got.reshape(halves)
        send = (pick(held, 1 - mine) + pick(got, 1 - mine).astype(F32)).astype(BF16)
        held = pick(held, mine) + pick(got, mine).astype(F32)
        got = exchange(send, lambda g, t: (g, t ^ (1 << orders[t % 2][j])))
    held, got = held[0], got[0]
    total = held + got.astype(F32)
    step = 1
    while step < groups:
        send = total.astype(BF16)
        got = exchange(send, lambda g, t: (g ^ step, t))
        total = send.astype(F32) + got.astype(F32)
        step *= 2
    return total * (1.0 / math.sqrt(lat * lon * groups * tiles))


def solution(mesh):
    groups, tiles = mesh.shape["grp"], mesh.shape["tile"]
    placed = (P("tile", "grp", None), P("tile", "grp", None), P(None, "tile", "grp"), P())
    return jax.shard_map(
        functools.partial(per_device, groups, tiles),
        mesh=mesh, in_specs=placed, out_specs=P("tile", None), check_vma=False,
    )
```

```python
import functools
import math

import jax
import jax.numpy as jnp
from jax import lax
from jax.experimental import pallas as pl
from jax.experimental.pallas import tpu as pltpu
from jax.sharding import PartitionSpec as P

F32 = jnp.float32
BF16 = jnp.bfloat16
AXES = ("grp", "tile")
IN_HBM = pl.BlockSpec(memory_space=pltpu.HBM)
IN_VMEM = pl.BlockSpec(memory_space=pltpu.VMEM)
KERNEL_VMEM = 24 << 20
WORD_CHUNK = 512
CHUNKS = 2


def project_kernel(occ_hbm, feat_hbm, basis_hbm, masked, proj, *rest):
    *edges, basis, total, occ, sems = rest
    row_a, row_b = edges[:2]
    lat, lon, words = masked.shape
    blocks = occ.shape[2]
    block = words // blocks
    chunk = min(WORD_CHUNK, words)
    count = words // chunk
    occ_copy = pltpu.make_async_copy(occ_hbm, occ, sems.at[2 * count])
    occ_copy.start()
    copies = []
    for k in range(count):
        part = pl.ds(k * chunk, chunk)
        basis_copy = pltpu.make_async_copy(basis_hbm.at[part], basis.at[part], sems.at[count + k])
        feat_copy = pltpu.make_async_copy(feat_hbm.at[:, :, part], masked.at[:, :, part], sems.at[k])
        basis_copy.start()
        feat_copy.start()
        copies.append((basis_copy, feat_copy))
    occ_copy.wait()
    for k in range(count):
        copies[k][0].wait()
        copies[k][1].wait()
        for i in range(lat // 2):
            for b in range(k * chunk // block, (k + 1) * chunk // block):
                gate = occ[i, 0, b].astype(F32).astype(BF16)
                spot = (pl.ds(2 * i, 2), slice(None), pl.ds(b * block, block))
                masked[spot] = masked[spot] * gate
        part = pl.ds(k * chunk, chunk)
        term = jnp.dot(
            masked[:, :, part].reshape(lat * lon, chunk), basis[part, :], preferred_element_type=F32
        )
        if k:
            term = total[...] + term
        if k < count - 1:
            total[...] = term
    rounded = term.astype(BF16)
    proj[...] = rounded.reshape(proj.shape)
    north, south = rounded[:lon], rounded[-lon:]
    even = lax.rem(lax.axis_index("tile"), 2) == 0
    row_a[...] = jnp.where(even, south, north)
    row_b[...] = jnp.where(even, north, south)
    grid = term.reshape(lat, lon, -1)
    west, east = grid[:, 0, :], grid[:, lon - 1, :]
    even = lax.rem(lax.axis_index("grp"), 2) == 0
    edges[2][...] = jnp.where(even, east, west).astype(BF16)
    if len(edges) > 3:
        edges[3][...] = jnp.where(even, west, east).astype(BF16)


def project(occupancy, features, basis_cols, columns):
    lat, lon, words = features.shape
    rank = basis_cols.shape[1]
    count = words // min(WORD_CHUNK, words)
    operands = [pltpu.with_memory_space_constraint(v, pltpu.HBM) for v in (occupancy, features, basis_cols)]
    return pl.pallas_call(
        project_kernel,
        out_shape=(
            pltpu.VMEM((lat, lon, words), BF16),
            pltpu.VMEM((lat, lon, rank), BF16),
            pltpu.VMEM((lon, rank), BF16),
            pltpu.VMEM((lon, rank), BF16),
        ) + (pltpu.VMEM((lat, rank), BF16),) * columns,
        in_specs=[IN_HBM] * 3,
        out_specs=(IN_VMEM,) * (4 + columns),
        scratch_shapes=[
            pltpu.VMEM(basis_cols.shape, BF16),
            pltpu.VMEM((lat * lon, rank), F32),
            pltpu.SMEM(occupancy.shape, jnp.int32),
            pltpu.SemaphoreType.DMA((2 * count + 1,)),
        ],
        compiler_params=pltpu.CompilerParams(vmem_limit_bytes=KERNEL_VMEM),
        cost_estimate=pl.CostEstimate(
            flops=2 * lat * lon * words * rank, bytes_accessed=2 * lat * lon * words, transcendentals=0
        ),
    )(*operands)


def smooth_rows(proj, north, south, west, east, links, smooth):
    lat, lon, rank = proj.shape
    weights = links[...].astype(F32)
    weights = weights / jnp.maximum(jnp.sum(weights, axis=0), 1.0)
    columns = [jnp.transpose(weights[k]) for k in range(4)]
    place = lax.broadcasted_iota(jnp.int32, (lon, rank), 0)
    for i in range(lat):
        row = proj[i].astype(F32)
        above = proj[i - 1].astype(F32) if i else north
        below = proj[i + 1].astype(F32) if i < lat - 1 else south
        left = jnp.where(place == 0, west[i:i + 1, :], pltpu.roll(row, 1, 0))
        right = jnp.where(place == lon - 1, east[i:i + 1, :], pltpu.roll(row, lon - 1, 0))
        link = [jnp.broadcast_to(columns[k][:, i:i + 1], (lon, rank)) for k in range(4)]
        value = link[0] * above + link[1] * below + link[2] * left + link[3] * right
        smooth[pl.ds(i * lon, lon), :] = value.astype(BF16)


def block_of(order, half, slot):
    steps = len(order)
    tile = sum(((slot >> (steps - 1 - j)) & 1) << bit for j, bit in enumerate(order))
    return tile + (half ^ (bin(tile).count("1") & 1))


def half_blocks(orders, sent, masked, values, outs):
    lat, lon, words = masked.shape
    slots, rows = outs[0].shape[:2]
    share = rows * len(outs)
    half = tile_parity() ^ sent
    contract = (((0,), (0,)), ((), ()))

    def put(slot, term):
        for k, out in enumerate(outs):
            out[slot] = term[k * rows:(k + 1) * rows].astype(out.dtype)

    if share % 128 == 0:
        count = max(1, 256 // share)
        for slot in range(0, slots, count):
            parts = []
            for at in range(slot, slot + count):
                first = jnp.where(half == 0, block_of(orders[0], 0, at), block_of(orders[1], 1, at)) * share
                part = masked[:, :, pl.ds(pl.multiple_of(first, share), share)]
                parts.append(part.reshape(lat * lon, share))
            part = jnp.concatenate(parts, axis=1) if count > 1 else parts[0]
            term = lax.dot_general(part, values, contract, preferred_element_type=F32)
            for at in range(count):
                put(slot + at, term[at * share:(at + 1) * share])
        return
    slot_of = [{block_of(order, h, at) // 2: at for at in range(slots)} for h, order in enumerate(orders)]
    step = 256
    for first in range(0, words, step):
        part = masked[:, :, pl.ds(first, step)].reshape(lat * lon, step)
        term = lax.dot_general(part, values, contract, preferred_element_type=F32)
        for at in range(0, step, 2 * share):
            pair = (first + at) // (2 * share)
            odd = bin(pair).count("1") & 1
            low, high = term[at:at + share], term[at + share:at + 2 * share]
            put(jnp.where(half == 0, slot_of[0][pair], slot_of[1][pair]), jnp.where(half == odd, low, high))


def tile_parity():
    tile = lax.axis_index("tile")
    parity = lax.rem(tile, 2)
    for bit in range(1, (lax.axis_size("tile") - 1).bit_length()):
        parity = parity ^ lax.rem(lax.shift_right_logical(tile, bit), 2)
    return parity


def partial_kernel(orders, masked, proj, halo_row_a, halo_row_b, *rest):
    *rest, smooth = rest
    rest, sends, keeps = rest[:-2 * CHUNKS], rest[-2 * CHUNKS:-CHUNKS], rest[-CHUNKS:]
    *halo_cols, links = rest
    row_a, row_b = halo_row_a[...].astype(F32), halo_row_b[...].astype(F32)
    odd = lax.rem(lax.axis_index("tile"), 2)
    north = jnp.where(odd == 0, row_b, row_a)
    south = jnp.where(odd == 0, row_a, row_b)
    col_a = halo_cols[0][...].astype(F32)
    col_b = halo_cols[1][...].astype(F32) if len(halo_cols) > 1 else jnp.zeros_like(col_a)
    even = lax.rem(lax.axis_index("grp"), 2) == 0
    west = jnp.where(even, col_b, col_a)
    east = jnp.where(even, col_a, col_b)
    smooth_rows(proj, north, south, west, east, links, smooth)
    values = smooth[...]
    half_blocks(orders, 1, masked, values, sends)
    half_blocks(orders, 0, masked, values, keeps)


def partial_product(orders, share, masked, proj, rows, cols, link_weights):
    lat, lon, words = masked.shape
    rank = proj.shape[2]
    shape = (words // share // 2, share // CHUNKS, rank)
    outs = pl.pallas_call(
        functools.partial(partial_kernel, orders),
        out_shape=(pltpu.VMEM(shape, BF16),) * CHUNKS + (pltpu.VMEM(shape, F32),) * CHUNKS,
        in_specs=[IN_VMEM] * (5 + len(cols)),
        out_specs=(IN_VMEM,) * (2 * CHUNKS),
        scratch_shapes=[pltpu.VMEM((lat * lon, rank), BF16)],
        compiler_params=pltpu.CompilerParams(vmem_limit_bytes=KERNEL_VMEM),
        cost_estimate=pl.CostEstimate(
            flops=2 * lat * lon * words * rank, bytes_accessed=2 * lat * lon * words, transcendentals=0
        ),
    )(masked, proj, *rows, *cols, link_weights)
    return outs[:CHUNKS], outs[CHUNKS:]


def bit_orders(bits):
    plain = list(range(1, bits))
    turned = plain[1::-1] + plain[2:]
    return plain, turned


def per_device(groups, tiles, features, occupancy, link_weights, basis_cols):
    lat, lon, words = features.shape
    share = words // tiles
    bits = tiles.bit_length() - 1
    orders = bit_orders(bits)
    tile = lax.axis_index("tile")

    def exchange(values, partner):
        pairs = []
        for g in range(groups):
            for t in range(tiles):
                to_g, to_t = partner(g, t)
                if 0 <= to_g < groups and 0 <= to_t < tiles:
                    pairs.append((g * tiles + t, to_g * tiles + to_t))
        return lax.ppermute(values, AXES, pairs)

    masked, proj, row_a, row_b, *cols = project(occupancy, features, basis_cols, 1 if groups <= 2 else 2)
    halo_row_b = exchange(row_b, lambda g, t: (g, t - 1 + 2 * (t % 2)))
    halo_cols = [exchange(cols[0], lambda g, t: (g + 1 - 2 * (g % 2), t))]
    if groups > 2:
        halo_cols.append(exchange(cols[1], lambda g, t: (g - 1 + 2 * (g % 2), t)))
    halo_row_a = exchange(row_a, lambda g, t: (g, t ^ 1))
    sends, keeps = partial_product(
        orders, share, masked, proj, (halo_row_a, halo_row_b), halo_cols, link_weights
    )
    parity = tile_parity()
    pick = functools.partial(lax.dynamic_index_in_dim, axis=0, keepdims=False)

    def reduced(held, send):
        got = exchange(send, lambda g, t: (g, t ^ 1))
        for j in range(bits - 1):
            bit = jnp.where(parity == 0, orders[0][j], orders[1][j])
            mine = lax.rem(lax.shift_right_logical(tile, bit), 2)
            halves = (2, held.shape[0] // 2) + held.shape[1:]
            held, got = held.reshape(halves), got.reshape(halves)
            send = (pick(held, 1 - mine) + pick(got, 1 - mine).astype(F32)).astype(BF16)
            held = pick(held, mine) + pick(got, mine).astype(F32)
            got = exchange(send, lambda g, t: (g, t ^ (1 << orders[bin(t).count("1") & 1][j]) ^ 1))
        total = held[0] + got[0].astype(F32)
        step = 1
        while step < groups:
            send = total.astype(BF16)
            got = exchange(send, lambda g, t: (g ^ step, t))
            total = send.astype(F32) + got.astype(F32)
            step *= 2
        return total * (1.0 / math.sqrt(lat * lon * groups * tiles))

    return jnp.concatenate([reduced(held, send) for held, send in zip(keeps, sends)], axis=0)


def solution(mesh):
    groups, tiles = mesh.shape["grp"], mesh.shape["tile"]
    placed = (P("tile", "grp", None), P("tile", "grp", None), P(None, "tile", "grp"), P())
    return jax.shard_map(
        functools.partial(per_device, groups, tiles),
        mesh=mesh, in_specs=placed, out_specs=P("tile", None), check_vma=False,
    )
```

```python
import functools
import math

import jax
import jax.numpy as jnp
from jax import lax
from jax.experimental import pallas as pl
from jax.experimental.pallas import tpu as pltpu
from jax.sharding import PartitionSpec as P

F32 = jnp.float32
BF16 = jnp.bfloat16
AXES = ("grp", "tile")
IN_HBM = pl.BlockSpec(memory_space=pltpu.HBM)
IN_VMEM = pl.BlockSpec(memory_space=pltpu.VMEM)
KERNEL_VMEM = 24 << 20
WORD_CHUNK = 512
CHUNKS = 2


def project_kernel(occ_hbm, feat_hbm, basis_hbm, masked, proj, *rest):
    *edges, basis, total, occ, sems = rest
    row_a, row_b = edges[:2]
    lat, lon, words = masked.shape
    blocks = occ.shape[2]
    block = words // blocks
    chunk = min(WORD_CHUNK, words)
    count = words // chunk
    occ_copy = pltpu.make_async_copy(occ_hbm, occ, sems.at[2 * count])
    occ_copy.start()
    copies = []
    for k in range(count):
        part = pl.ds(k * chunk, chunk)
        basis_copy = pltpu.make_async_copy(basis_hbm.at[part], basis.at[part], sems.at[count + k])
        feat_copy = pltpu.make_async_copy(feat_hbm.at[:, :, part], masked.at[:, :, part], sems.at[k])
        basis_copy.start()
        feat_copy.start()
        copies.append((basis_copy, feat_copy))
    occ_copy.wait()
    for k in range(count):
        copies[k][0].wait()
        copies[k][1].wait()
        for i in range(lat // 2):
            for b in range(k * chunk // block, (k + 1) * chunk // block):
                gate = occ[i, 0, b].astype(F32).astype(BF16)
                spot = (pl.ds(2 * i, 2), slice(None), pl.ds(b * block, block))
                masked[spot] = masked[spot] * gate
        part = pl.ds(k * chunk, chunk)
        term = jnp.dot(
            masked[:, :, part].reshape(lat * lon, chunk), basis[part, :], preferred_element_type=F32
        )
        if k:
            term = total[...] + term
        if k < count - 1:
            total[...] = term
    rounded = term.astype(BF16)
    proj[...] = rounded.reshape(proj.shape)
    north, south = rounded[:lon], rounded[-lon:]
    even = lax.rem(lax.axis_index("tile"), 2) == 0
    row_a[...] = jnp.where(even, south, north)
    row_b[...] = jnp.where(even, north, south)
    grid = term.reshape(lat, lon, -1)
    west, east = grid[:, 0, :], grid[:, lon - 1, :]
    even = lax.rem(lax.axis_index("grp"), 2) == 0
    edges[2][...] = jnp.where(even, east, west).astype(BF16)
    if len(edges) > 3:
        edges[3][...] = jnp.where(even, west, east).astype(BF16)


def project(occupancy, features, basis_cols, columns):
    lat, lon, words = features.shape
    rank = basis_cols.shape[1]
    count = words // min(WORD_CHUNK, words)
    operands = [pltpu.with_memory_space_constraint(v, pltpu.HBM) for v in (occupancy, features, basis_cols)]
    return pl.pallas_call(
        project_kernel,
        out_shape=(
            pltpu.VMEM((lat, lon, words), BF16),
            pltpu.VMEM((lat, lon, rank), BF16),
            pltpu.VMEM((lon, rank), BF16),
            pltpu.VMEM((lon, rank), BF16),
        ) + (pltpu.VMEM((lat, rank), BF16),) * columns,
        in_specs=[IN_HBM] * 3,
        out_specs=(IN_VMEM,) * (4 + columns),
        scratch_shapes=[
            pltpu.VMEM(basis_cols.shape, BF16),
            pltpu.VMEM((lat * lon, rank), F32),
            pltpu.SMEM(occupancy.shape, jnp.int32),
            pltpu.SemaphoreType.DMA((2 * count + 1,)),
        ],
        compiler_params=pltpu.CompilerParams(vmem_limit_bytes=KERNEL_VMEM),
        cost_estimate=pl.CostEstimate(
            flops=2 * lat * lon * words * rank, bytes_accessed=2 * lat * lon * words, transcendentals=0
        ),
    )(*operands)


def smooth_rows(proj, north, south, west, east, links, smooth):
    lat, lon, rank = proj.shape
    weights = links[...].astype(F32)
    weights = weights / jnp.maximum(jnp.sum(weights, axis=0), 1.0)
    columns = [jnp.transpose(weights[k]) for k in range(4)]
    place = lax.broadcasted_iota(jnp.int32, (lon, rank), 0)
    for i in range(lat):
        row = proj[i].astype(F32)
        above = proj[i - 1].astype(F32) if i else north
        below = proj[i + 1].astype(F32) if i < lat - 1 else south
        left = jnp.where(place == 0, west[i:i + 1, :], pltpu.roll(row, 1, 0))
        right = jnp.where(place == lon - 1, east[i:i + 1, :], pltpu.roll(row, lon - 1, 0))
        link = [jnp.broadcast_to(columns[k][:, i:i + 1], (lon, rank)) for k in range(4)]
        value = link[0] * above + link[1] * below + link[2] * left + link[3] * right
        smooth[pl.ds(i * lon, lon), :] = value.astype(BF16)


def block_of(order, half, slot):
    steps = len(order)
    tile = sum(((slot >> (steps - 1 - j)) & 1) << bit for j, bit in enumerate(order))
    return tile + (half ^ (bin(tile).count("1") & 1))


def half_blocks(orders, sent, masked, values, outs):
    lat, lon, words = masked.shape
    slots, rows = outs[0].shape[:2]
    share = rows * len(outs)
    half = tile_parity() ^ sent
    contract = (((0,), (0,)), ((), ()))

    def put(slot, term):
        for k, out in enumerate(outs):
            out[slot] = term[k * rows:(k + 1) * rows].astype(out.dtype)

    if share % 128 == 0:
        count = max(1, 256 // share)
        for slot in range(0, slots, count):
            parts = []
            for at in range(slot, slot + count):
                first = jnp.where(half == 0, block_of(orders[0], 0, at), block_of(orders[1], 1, at)) * share
                part = masked[:, :, pl.ds(pl.multiple_of(first, share), share)]
                parts.append(part.reshape(lat * lon, share))
            part = jnp.concatenate(parts, axis=1) if count > 1 else parts[0]
            term = lax.dot_general(part, values, contract, preferred_element_type=F32)
            for at in range(count):
                put(slot + at, term[at * share:(at + 1) * share])
        return
    slot_of = [{block_of(order, h, at) // 2: at for at in range(slots)} for h, order in enumerate(orders)]
    step = 256
    for first in range(0, words, step):
        part = masked[:, :, pl.ds(first, step)].reshape(lat * lon, step)
        term = lax.dot_general(part, values, contract, preferred_element_type=F32)
        for at in range(0, step, 2 * share):
            pair = (first + at) // (2 * share)
            odd = bin(pair).count("1") & 1
            low, high = term[at:at + share], term[at + share:at + 2 * share]
            put(jnp.where(half == 0, slot_of[0][pair], slot_of[1][pair]), jnp.where(half == odd, low, high))


def tile_parity():
    tile = lax.axis_index("tile")
    parity = lax.rem(tile, 2)
    for bit in range(1, (lax.axis_size("tile") - 1).bit_length()):
        parity = parity ^ lax.rem(lax.shift_right_logical(tile, bit), 2)
    return parity


def ends(axis):
    place = lax.axis_index(axis)
    return place == 0, place == lax.axis_size(axis) - 1


def partial_kernel(orders, masked, proj, halo_row_a, halo_row_b, *rest):
    *rest, smooth = rest
    rest, sends, keeps = rest[:-2 * CHUNKS], rest[-2 * CHUNKS:-CHUNKS], rest[-CHUNKS:]
    *halo_cols, links = rest
    row_a, row_b = halo_row_a[...].astype(F32), halo_row_b[...].astype(F32)
    odd = lax.rem(lax.axis_index("tile"), 2)
    first, last = ends("tile")
    north = jnp.where(first, 0.0, jnp.where(odd == 0, row_b, row_a))
    south = jnp.where(last, 0.0, jnp.where(odd == 0, row_a, row_b))
    col_a = halo_cols[0][...].astype(F32)
    col_b = halo_cols[1][...].astype(F32) if len(halo_cols) > 1 else jnp.zeros_like(col_a)
    even = lax.rem(lax.axis_index("grp"), 2) == 0
    first, last = ends("grp")
    west = jnp.where(first, 0.0, jnp.where(even, col_b, col_a))
    east = jnp.where(last, 0.0, jnp.where(even, col_a, col_b))
    smooth_rows(proj, north, south, west, east, links, smooth)
    values = smooth[...]
    half_blocks(orders, 1, masked, values, sends)
    half_blocks(orders, 0, masked, values, keeps)


def partial_product(orders, share, masked, proj, rows, cols, link_weights):
    lat, lon, words = masked.shape
    rank = proj.shape[2]
    shape = (words // share // 2, share // CHUNKS, rank)
    outs = pl.pallas_call(
        functools.partial(partial_kernel, orders),
        out_shape=(pltpu.VMEM(shape, BF16),) * CHUNKS + (pltpu.VMEM(shape, F32),) * CHUNKS,
        in_specs=[IN_VMEM] * (5 + len(cols)),
        out_specs=(IN_VMEM,) * (2 * CHUNKS),
        scratch_shapes=[pltpu.VMEM((lat * lon, rank), BF16)],
        compiler_params=pltpu.CompilerParams(vmem_limit_bytes=KERNEL_VMEM),
        cost_estimate=pl.CostEstimate(
            flops=2 * lat * lon * words * rank, bytes_accessed=2 * lat * lon * words, transcendentals=0
        ),
    )(masked, proj, *rows, *cols, link_weights)
    return outs[:CHUNKS], outs[CHUNKS:]


def bit_orders(bits):
    plain = list(range(1, bits))
    turned = plain[1::-1] + plain[2:]
    return plain, turned


def per_device(groups, tiles, features, occupancy, link_weights, basis_cols):
    lat, lon, words = features.shape
    share = words // tiles
    bits = tiles.bit_length() - 1
    orders = bit_orders(bits)
    tile = lax.axis_index("tile")

    def exchange(values, partner):
        pairs = []
        for g in range(groups):
            for t in range(tiles):
                to_g, to_t = partner(g, t)
                if not 0 <= to_t < tiles:
                    to_g, to_t = g ^ 1, t
                pairs.append((g * tiles + t, to_g % groups * tiles + to_t))
        return lax.ppermute(values, AXES, pairs)

    masked, proj, row_a, row_b, *cols = project(occupancy, features, basis_cols, 1 if groups <= 2 else 2)
    halo_row_b = exchange(row_b, lambda g, t: (g, t - 1 + 2 * (t % 2)))
    halo_cols = [exchange(cols[0], lambda g, t: (g + 1 - 2 * (g % 2), t))]
    if groups > 2:
        halo_cols.append(exchange(cols[1], lambda g, t: (g - 1 + 2 * (g % 2), t)))
    halo_row_a = exchange(row_a, lambda g, t: (g, t ^ 1))
    sends, keeps = partial_product(
        orders, share, masked, proj, (halo_row_a, halo_row_b), halo_cols, link_weights
    )
    parity = tile_parity()
    pick = functools.partial(lax.dynamic_index_in_dim, axis=0, keepdims=False)

    def reduced(held, send):
        got = exchange(send, lambda g, t: (g, t ^ 1))
        for j in range(bits - 1):
            bit = jnp.where(parity == 0, orders[0][j], orders[1][j])
            mine = lax.rem(lax.shift_right_logical(tile, bit), 2)
            halves = (2, held.shape[0] // 2) + held.shape[1:]
            held, got = held.reshape(halves), got.reshape(halves)
            send = (pick(held, 1 - mine) + pick(got, 1 - mine).astype(F32)).astype(BF16)
            held = pick(held, mine) + pick(got, mine).astype(F32)
            got = exchange(send, lambda g, t: (g, t ^ (1 << orders[bin(t).count("1") & 1][j]) ^ 1))
        total = held[0] + got[0].astype(F32)
        step = 1
        while step < groups:
            send = total.astype(BF16)
            got = exchange(send, lambda g, t: (g ^ step, t))
            total = send.astype(F32) + got.astype(F32)
            step *= 2
        return total * (1.0 / math.sqrt(lat * lon * groups * tiles))

    return jnp.concatenate([reduced(held, send) for held, send in zip(keeps, sends)], axis=0)


def solution(mesh):
    groups, tiles = mesh.shape["grp"], mesh.shape["tile"]
    placed = (P("tile", "grp", None), P("tile", "grp", None), P(None, "tile", "grp"), P())
    return jax.shard_map(
        functools.partial(per_device, groups, tiles),
        mesh=mesh, in_specs=placed, out_specs=P("tile", None), check_vma=False,
    )
```

```python
import functools
import math

import jax
import jax.numpy as jnp
from jax import lax
from jax.experimental import pallas as pl
from jax.experimental.pallas import tpu as pltpu
from jax.sharding import PartitionSpec as P

F32 = jnp.float32
BF16 = jnp.bfloat16
AXES = ("grp", "tile")
IN_HBM = pl.BlockSpec(memory_space=pltpu.HBM)
IN_VMEM = pl.BlockSpec(memory_space=pltpu.VMEM)
KERNEL_VMEM = 24 << 20
WORD_CHUNKS = (0.375, 0.375, 0.25)
CHUNKS = 2


def word_chunks(words):
    sizes = [int(words * part) for part in WORD_CHUNKS]
    return [(sum(sizes[:k]), size) for k, size in enumerate(sizes)]


def project_kernel(occ_hbm, links_hbm, feat_hbm, basis_hbm, masked, proj, shares, *rest):
    *edges, basis, total, links, occ, sems = rest
    row_a, row_b = edges[:2]
    lat, lon, words = masked.shape
    block = words // occ.shape[2]
    chunks = word_chunks(words)
    count = len(chunks)
    links_copy = pltpu.make_async_copy(links_hbm, links, sems.at[2 * count])
    occ_copy = pltpu.make_async_copy(occ_hbm, occ, sems.at[2 * count + 1])
    links_copy.start()
    occ_copy.start()
    copies = []
    for k, (start, size) in enumerate(chunks):
        part = pl.ds(start, size)
        basis_copy = pltpu.make_async_copy(basis_hbm.at[part], basis.at[part], sems.at[count + k])
        feat_copy = pltpu.make_async_copy(feat_hbm.at[:, :, part], masked.at[:, :, part], sems.at[k])
        basis_copy.start()
        feat_copy.start()
        copies.append((basis_copy, feat_copy))
    links_copy.wait()
    weights = links[...].astype(F32)
    weights = weights / jnp.maximum(jnp.sum(weights, axis=0), 1.0)
    for k in range(4):
        column = jnp.transpose(weights[k])
        for i in range(lat):
            shares[k, pl.ds(i * lon, lon), :] = jnp.broadcast_to(column[:, i:i + 1], (lon, shares.shape[2]))
    occ_copy.wait()
    for k, (start, size) in enumerate(chunks):
        copies[k][0].wait()
        copies[k][1].wait()
        for i in range(lat // 2):
            for b in range(start // block, (start + size) // block):
                gate = occ[i, 0, b].astype(F32).astype(BF16)
                spot = (pl.ds(2 * i, 2), slice(None), pl.ds(b * block, block))
                masked[spot] = masked[spot] * gate
        part = pl.ds(start, size)
        term = jnp.dot(
            masked[:, :, part].reshape(lat * lon, size), basis[part, :], preferred_element_type=F32
        )
        if k:
            term = total[...] + term
        if k < count - 1:
            total[...] = term
    rounded = term.astype(BF16)
    proj[...] = rounded.reshape(proj.shape)
    north, south = rounded[:lon], rounded[-lon:]
    even = lax.rem(lax.axis_index("tile"), 2) == 0
    row_a[...] = jnp.where(even, south, north)
    row_b[...] = jnp.where(even, north, south)
    grid = term.reshape(lat, lon, -1)
    west, east = grid[:, 0, :], grid[:, lon - 1, :]
    even = lax.rem(lax.axis_index("grp"), 2) == 0
    edges[2][...] = jnp.where(even, east, west).astype(BF16)
    if len(edges) > 3:
        edges[3][...] = jnp.where(even, west, east).astype(BF16)


def project(occupancy, link_weights, features, basis_cols, columns):
    lat, lon, words = features.shape
    rank = basis_cols.shape[1]
    operands = [
        pltpu.with_memory_space_constraint(v, pltpu.HBM)
        for v in (occupancy, link_weights, features, basis_cols)
    ]
    return pl.pallas_call(
        project_kernel,
        out_shape=(
            pltpu.VMEM((lat, lon, words), BF16),
            pltpu.VMEM((lat, lon, rank), BF16),
            pltpu.VMEM((4, lat * lon, min(rank, 128)), F32),
            pltpu.VMEM((lon, rank), BF16),
            pltpu.VMEM((lon, rank), BF16),
        ) + (pltpu.VMEM((lat, rank), BF16),) * columns,
        in_specs=[IN_HBM] * 4,
        out_specs=(IN_VMEM,) * (5 + columns),
        scratch_shapes=[
            pltpu.VMEM(basis_cols.shape, BF16),
            pltpu.VMEM((lat * lon, rank), F32),
            pltpu.VMEM(link_weights.shape, jnp.int32),
            pltpu.SMEM(occupancy.shape, jnp.int32),
            pltpu.SemaphoreType.DMA((2 * len(word_chunks(words)) + 2,)),
        ],
        compiler_params=pltpu.CompilerParams(vmem_limit_bytes=KERNEL_VMEM),
        cost_estimate=pl.CostEstimate(
            flops=2 * lat * lon * words * rank, bytes_accessed=2 * lat * lon * words, transcendentals=0
        ),
    )(*operands)


def smooth_rows(proj, north, south, west, east, shares, smooth):
    lat, lon, rank = proj.shape
    wide = rank // shares.shape[2]
    place = lax.broadcasted_iota(jnp.int32, (lon, rank), 0)
    for i in range(lat):
        row = proj[i].astype(F32)
        above = proj[i - 1].astype(F32) if i else north
        below = proj[i + 1].astype(F32) if i < lat - 1 else south
        left = jnp.where(place == 0, west[i:i + 1, :], pltpu.roll(row, 1, 0))
        right = jnp.where(place == lon - 1, east[i:i + 1, :], pltpu.roll(row, lon - 1, 0))
        link = [jnp.tile(shares[k, pl.ds(i * lon, lon), :], (1, wide)) for k in range(4)]
        value = link[0] * above + link[1] * below + link[2] * left + link[3] * right
        smooth[pl.ds(i * lon, lon), :] = value.astype(BF16)


def block_of(order, half, slot):
    steps = len(order)
    tile = sum(((slot >> (steps - 1 - j)) & 1) << bit for j, bit in enumerate(order))
    return tile + (half ^ (bin(tile).count("1") & 1))


def half_blocks(orders, sent, masked, values, outs):
    lat, lon, words = masked.shape
    slots, rows = outs[0].shape[:2]
    share = rows * len(outs)
    half = tile_parity() ^ sent
    contract = (((0,), (0,)), ((), ()))

    def put(slot, term):
        for k, out in enumerate(outs):
            out[slot] = term[k * rows:(k + 1) * rows].astype(out.dtype)

    if share % 128 == 0:
        count = max(1, 256 // share)
        for slot in range(0, slots, count):
            parts = []
            for at in range(slot, slot + count):
                first = jnp.where(half == 0, block_of(orders[0], 0, at), block_of(orders[1], 1, at)) * share
                part = masked[:, :, pl.ds(pl.multiple_of(first, share), share)]
                parts.append(part.reshape(lat * lon, share))
            part = jnp.concatenate(parts, axis=1) if count > 1 else parts[0]
            term = lax.dot_general(part, values, contract, preferred_element_type=F32)
            for at in range(count):
                put(slot + at, term[at * share:(at + 1) * share])
        return
    slot_of = [{block_of(order, h, at) // 2: at for at in range(slots)} for h, order in enumerate(orders)]
    step = 256
    for first in range(0, words, step):
        part = masked[:, :, pl.ds(first, step)].reshape(lat * lon, step)
        term = lax.dot_general(part, values, contract, preferred_element_type=F32)
        for at in range(0, step, 2 * share):
            pair = (first + at) // (2 * share)
            odd = bin(pair).count("1") & 1
            low, high = term[at:at + share], term[at + share:at + 2 * share]
            put(jnp.where(half == 0, slot_of[0][pair], slot_of[1][pair]), jnp.where(half == odd, low, high))


def tile_parity():
    tile = lax.axis_index("tile")
    parity = lax.rem(tile, 2)
    for bit in range(1, (lax.axis_size("tile") - 1).bit_length()):
        parity = parity ^ lax.rem(lax.shift_right_logical(tile, bit), 2)
    return parity


def ends(axis):
    place = lax.axis_index(axis)
    return place == 0, place == lax.axis_size(axis) - 1


def partial_kernel(orders, masked, proj, halo_row_a, halo_row_b, *rest):
    *rest, smooth = rest
    rest, sends, keeps = rest[:-2 * CHUNKS], rest[-2 * CHUNKS:-CHUNKS], rest[-CHUNKS:]
    *halo_cols, shares = rest
    row_a, row_b = halo_row_a[...].astype(F32), halo_row_b[...].astype(F32)
    odd = lax.rem(lax.axis_index("tile"), 2)
    first, last = ends("tile")
    north = jnp.where(first, 0.0, jnp.where(odd == 0, row_b, row_a))
    south = jnp.where(last, 0.0, jnp.where(odd == 0, row_a, row_b))
    col_a = halo_cols[0][...].astype(F32)
    col_b = halo_cols[1][...].astype(F32) if len(halo_cols) > 1 else jnp.zeros_like(col_a)
    even = lax.rem(lax.axis_index("grp"), 2) == 0
    first, last = ends("grp")
    west = jnp.where(first, 0.0, jnp.where(even, col_b, col_a))
    east = jnp.where(last, 0.0, jnp.where(even, col_a, col_b))
    smooth_rows(proj, north, south, west, east, shares, smooth)
    values = smooth[...]
    half_blocks(orders, 1, masked, values, sends)
    half_blocks(orders, 0, masked, values, keeps)


def partial_product(orders, share, masked, proj, rows, cols, shares):
    lat, lon, words = masked.shape
    rank = proj.shape[2]
    shape = (words // share // 2, share // CHUNKS, rank)
    outs = pl.pallas_call(
        functools.partial(partial_kernel, orders),
        out_shape=(pltpu.VMEM(shape, BF16),) * CHUNKS + (pltpu.VMEM(shape, F32),) * CHUNKS,
        in_specs=[IN_VMEM] * (5 + len(cols)),
        out_specs=(IN_VMEM,) * (2 * CHUNKS),
        scratch_shapes=[pltpu.VMEM((lat * lon, rank), BF16)],
        compiler_params=pltpu.CompilerParams(vmem_limit_bytes=KERNEL_VMEM),
        cost_estimate=pl.CostEstimate(
            flops=2 * lat * lon * words * rank, bytes_accessed=2 * lat * lon * words, transcendentals=0
        ),
    )(masked, proj, *rows, *cols, shares)
    return outs[:CHUNKS], outs[CHUNKS:]


def bit_orders(bits):
    plain = list(range(1, bits))
    turned = plain[1::-1] + plain[2:]
    return plain, turned


def per_device(groups, tiles, features, occupancy, link_weights, basis_cols):
    lat, lon, words = features.shape
    share = words // tiles
    bits = tiles.bit_length() - 1
    orders = bit_orders(bits)
    tile = lax.axis_index("tile")

    def exchange(values, partner):
        pairs = []
        for g in range(groups):
            for t in range(tiles):
                to_g, to_t = partner(g, t)
                if not 0 <= to_t < tiles:
                    to_g, to_t = g ^ 1, t
                pairs.append((g * tiles + t, to_g % groups * tiles + to_t))
        return lax.ppermute(values, AXES, pairs)

    masked, proj, shares, row_a, row_b, *cols = project(
        occupancy, link_weights, features, basis_cols, 1 if groups <= 2 else 2
    )
    halo_row_b = exchange(row_b, lambda g, t: (g, t - 1 + 2 * (t % 2)))
    halo_cols = [exchange(cols[0], lambda g, t: (g + 1 - 2 * (g % 2), t))]
    if groups > 2:
        halo_cols.append(exchange(cols[1], lambda g, t: (g - 1 + 2 * (g % 2), t)))
    halo_row_a = exchange(row_a, lambda g, t: (g, t ^ 1))
    sends, keeps = partial_product(
        orders, share, masked, proj, (halo_row_a, halo_row_b), halo_cols, shares
    )
    parity = tile_parity()
    pick = functools.partial(lax.dynamic_index_in_dim, axis=0, keepdims=False)

    def reduced(held, send):
        got = exchange(send, lambda g, t: (g, t ^ 1))
        for j in range(bits - 1):
            bit = jnp.where(parity == 0, orders[0][j], orders[1][j])
            mine = lax.rem(lax.shift_right_logical(tile, bit), 2)
            halves = (2, held.shape[0] // 2) + held.shape[1:]
            held, got = held.reshape(halves), got.reshape(halves)
            send = (pick(held, 1 - mine) + pick(got, 1 - mine).astype(F32)).astype(BF16)
            held = pick(held, mine) + pick(got, mine).astype(F32)
            got = exchange(send, lambda g, t: (g, t ^ (1 << orders[bin(t).count("1") & 1][j]) ^ 1))
        total = held[0] + got[0].astype(F32)
        step = 1
        while step < groups:
            send = total.astype(BF16)
            got = exchange(send, lambda g, t: (g ^ step, t))
            total = send.astype(F32) + got.astype(F32)
            step *= 2
        return total * (1.0 / math.sqrt(lat * lon * groups * tiles))

    return jnp.concatenate([reduced(held, send) for held, send in zip(keeps, sends)], axis=0)


def solution(mesh):
    groups, tiles = mesh.shape["grp"], mesh.shape["tile"]
    placed = (P("tile", "grp", None), P("tile", "grp", None), P(None, "tile", "grp"), P())
    return jax.shard_map(
        functools.partial(per_device, groups, tiles),
        mesh=mesh, in_specs=placed, out_specs=P("tile", None), check_vma=False,
    )
```

```python
import functools
import math

import jax
import jax.numpy as jnp
from jax import lax
from jax.experimental import pallas as pl
from jax.experimental.pallas import tpu as pltpu
from jax.sharding import PartitionSpec as P

F32 = jnp.float32
BF16 = jnp.bfloat16
AXES = ("grp", "tile")
IN_HBM = pl.BlockSpec(memory_space=pltpu.HBM)
IN_VMEM = pl.BlockSpec(memory_space=pltpu.VMEM)
KERNEL_VMEM = 24 << 20
WORD_CHUNKS = (0.375, 0.375, 0.25)


def word_chunks(words):
    sizes = [int(words * part) for part in WORD_CHUNKS]
    return [(sum(sizes[:k]), size) for k, size in enumerate(sizes)]


def project_kernel(occ_hbm, links_hbm, feat_hbm, basis_hbm, masked, proj, shares, *rest):
    *edges, basis, total, links, occ, sems = rest
    row_a, row_b = edges[:2]
    lat, lon, words = masked.shape
    block = words // occ.shape[2]
    chunks = word_chunks(words)
    count = len(chunks)
    links_copy = pltpu.make_async_copy(links_hbm, links, sems.at[2 * count])
    occ_copy = pltpu.make_async_copy(occ_hbm, occ, sems.at[2 * count + 1])
    links_copy.start()
    occ_copy.start()
    copies = []
    for k, (start, size) in enumerate(chunks):
        part = pl.ds(start, size)
        basis_copy = pltpu.make_async_copy(basis_hbm.at[part], basis.at[part], sems.at[count + k])
        feat_copy = pltpu.make_async_copy(feat_hbm.at[:, :, part], masked.at[:, :, part], sems.at[k])
        basis_copy.start()
        feat_copy.start()
        copies.append((basis_copy, feat_copy))
    links_copy.wait()
    weights = links[...].astype(F32)
    weights = weights / jnp.maximum(jnp.sum(weights, axis=0), 1.0)
    for k in range(4):
        column = jnp.transpose(weights[k])
        for i in range(lat):
            shares[k, pl.ds(i * lon, lon), :] = jnp.broadcast_to(column[:, i:i + 1], (lon, shares.shape[2]))
    occ_copy.wait()
    for k, (start, size) in enumerate(chunks):
        copies[k][0].wait()
        copies[k][1].wait()
        for i in range(lat // 2):
            for b in range(start // block, (start + size) // block):
                gate = occ[i, 0, b].astype(F32).astype(BF16)
                spot = (pl.ds(2 * i, 2), slice(None), pl.ds(b * block, block))
                masked[spot] = masked[spot] * gate
        part = pl.ds(start, size)
        term = jnp.dot(
            masked[:, :, part].reshape(lat * lon, size), basis[part, :], preferred_element_type=F32
        )
        if k:
            term = total[...] + term
        if k < count - 1:
            total[...] = term
    rounded = term.astype(BF16)
    proj[...] = rounded.reshape(proj.shape)
    north, south = rounded[:lon], rounded[-lon:]
    even = lax.rem(lax.axis_index("tile"), 2) == 0
    row_a[...] = jnp.where(even, south, north)
    row_b[...] = jnp.where(even, north, south)
    grid = term.reshape(lat, lon, -1)
    west, east = grid[:, 0, :], grid[:, lon - 1, :]
    even = lax.rem(lax.axis_index("grp"), 2) == 0
    edges[2][...] = jnp.where(even, east, west).astype(BF16)
    if len(edges) > 3:
        edges[3][...] = jnp.where(even, west, east).astype(BF16)


def project(occupancy, link_weights, features, basis_cols, columns):
    lat, lon, words = features.shape
    rank = basis_cols.shape[1]
    operands = [
        pltpu.with_memory_space_constraint(v, pltpu.HBM)
        for v in (occupancy, link_weights, features, basis_cols)
    ]
    return pl.pallas_call(
        project_kernel,
        out_shape=(
            pltpu.VMEM((lat, lon, words), BF16),
            pltpu.VMEM((lat, lon, rank), BF16),
            pltpu.VMEM((4, lat * lon, min(rank, 128)), F32),
            pltpu.VMEM((lon, rank), BF16),
            pltpu.VMEM((lon, rank), BF16),
        ) + (pltpu.VMEM((lat, rank), BF16),) * columns,
        in_specs=[IN_HBM] * 4,
        out_specs=(IN_VMEM,) * (5 + columns),
        scratch_shapes=[
            pltpu.VMEM(basis_cols.shape, BF16),
            pltpu.VMEM((lat * lon, rank), F32),
            pltpu.VMEM(link_weights.shape, jnp.int32),
            pltpu.SMEM(occupancy.shape, jnp.int32),
            pltpu.SemaphoreType.DMA((2 * len(word_chunks(words)) + 2,)),
        ],
        compiler_params=pltpu.CompilerParams(vmem_limit_bytes=KERNEL_VMEM),
        cost_estimate=pl.CostEstimate(
            flops=2 * lat * lon * words * rank, bytes_accessed=2 * lat * lon * words, transcendentals=0
        ),
    )(*operands)


def smooth_rows(proj, north, south, west, east, shares, smooth):
    lat, lon, rank = proj.shape
    wide = rank // shares.shape[2]
    place = lax.broadcasted_iota(jnp.int32, (lon, rank), 0)
    for i in range(lat):
        row = proj[i].astype(F32)
        above = proj[i - 1].astype(F32) if i else north
        below = proj[i + 1].astype(F32) if i < lat - 1 else south
        left = jnp.where(place == 0, west[i:i + 1, :], pltpu.roll(row, 1, 0))
        right = jnp.where(place == lon - 1, east[i:i + 1, :], pltpu.roll(row, lon - 1, 0))
        link = [jnp.tile(shares[k, pl.ds(i * lon, lon), :], (1, wide)) for k in range(4)]
        value = link[0] * above + link[1] * below + link[2] * left + link[3] * right
        smooth[pl.ds(i * lon, lon), :] = value.astype(BF16)


def block_of(order, half, slot):
    steps = len(order)
    tile = sum(((slot >> (steps - 1 - j)) & 1) << bit for j, bit in enumerate(order))
    return tile + (half ^ (bin(tile).count("1") & 1))


def half_blocks(orders, sent, masked, values, outs):
    lat, lon, words = masked.shape
    places, share = outs[0].shape[:2]
    tile = lax.axis_index("tile")
    half = tile_parity() ^ sent
    own = jnp.where(half == 0, tile_bit(tile, orders[0][-1]), tile_bit(tile, orders[1][-1]))
    contract = (((0,), (0,)), ((), ()))
    if share % 128 == 0:
        count = max(1, 256 // share)
        for forward, out in ((1, outs[0]), (0, outs[1])):
            last = own ^ forward
            for place in range(0, places, count):
                parts = []
                for at in range(place, place + count):
                    block = [[block_of(order, h, 2 * at + low) for low in (0, 1)] for h, order in enumerate(orders)]
                    first = jnp.where(
                        half == 0,
                        jnp.where(last == 0, block[0][0], block[0][1]),
                        jnp.where(last == 0, block[1][0], block[1][1]),
                    ) * share
                    part = masked[:, :, pl.ds(pl.multiple_of(first, share), share)]
                    parts.append(part.reshape(lat * lon, share))
                part = jnp.concatenate(parts, axis=1) if count > 1 else parts[0]
                term = lax.dot_general(part, values, contract, preferred_element_type=F32)
                out[pl.ds(place, count)] = term.astype(out.dtype).reshape(count, share, -1)
        return
    slot_of = [
        {block_of(order, h, at) // 2: at for at in range(2 * places)} for h, order in enumerate(orders)
    ]
    step = 256
    for first in range(0, words, step):
        part = masked[:, :, pl.ds(first, step)].reshape(lat * lon, step)
        term = lax.dot_general(part, values, contract, preferred_element_type=F32)
        for at in range(0, step, 2 * share):
            pair = (first + at) // (2 * share)
            odd = bin(pair).count("1") & 1
            low, high = term[at:at + share], term[at + share:at + 2 * share]
            value = jnp.where(half == odd, low, high)
            slot = jnp.where(half == 0, slot_of[0][pair], slot_of[1][pair])
            for forward, out in ((1, outs[0]), (0, outs[1])):

                @pl.when(lax.rem(slot, 2) == own ^ forward)
                def _():
                    out[lax.div(slot, 2)] = value.astype(out.dtype)


def tile_bit(tile, bit):
    return lax.rem(lax.shift_right_logical(tile, bit), 2)


def tile_parity():
    tile = lax.axis_index("tile")
    parity = lax.rem(tile, 2)
    for bit in range(1, (lax.axis_size("tile") - 1).bit_length()):
        parity = parity ^ tile_bit(tile, bit)
    return parity


def ends(axis):
    place = lax.axis_index(axis)
    return place == 0, place == lax.axis_size(axis) - 1


def partial_kernel(orders, masked, proj, halo_row_a, halo_row_b, *rest):
    *rest, smooth = rest
    rest, sends, keeps = rest[:-4], rest[-4:-2], rest[-2:]
    *halo_cols, shares = rest
    row_a, row_b = halo_row_a[...].astype(F32), halo_row_b[...].astype(F32)
    odd = lax.rem(lax.axis_index("tile"), 2)
    first, last = ends("tile")
    north = jnp.where(first, 0.0, jnp.where(odd == 0, row_b, row_a))
    south = jnp.where(last, 0.0, jnp.where(odd == 0, row_a, row_b))
    col_a = halo_cols[0][...].astype(F32)
    col_b = halo_cols[1][...].astype(F32) if len(halo_cols) > 1 else jnp.zeros_like(col_a)
    even = lax.rem(lax.axis_index("grp"), 2) == 0
    first, last = ends("grp")
    west = jnp.where(first, 0.0, jnp.where(even, col_b, col_a))
    east = jnp.where(last, 0.0, jnp.where(even, col_a, col_b))
    smooth_rows(proj, north, south, west, east, shares, smooth)
    values = smooth[...]
    half_blocks(orders, 1, masked, values, sends)
    half_blocks(orders, 0, masked, values, keeps)


def partial_product(orders, share, masked, proj, rows, cols, shares):
    lat, lon, words = masked.shape
    rank = proj.shape[2]
    shape = (words // share // 4, share, rank)
    outs = pl.pallas_call(
        functools.partial(partial_kernel, orders),
        out_shape=(pltpu.VMEM(shape, BF16),) * 2 + (pltpu.VMEM(shape, F32),) * 2,
        in_specs=[IN_VMEM] * (5 + len(cols)),
        out_specs=(IN_VMEM,) * 4,
        scratch_shapes=[pltpu.VMEM((lat * lon, rank), BF16)],
        compiler_params=pltpu.CompilerParams(vmem_limit_bytes=KERNEL_VMEM),
        cost_estimate=pl.CostEstimate(
            flops=2 * lat * lon * words * rank, bytes_accessed=2 * lat * lon * words, transcendentals=0
        ),
    )(masked, proj, *rows, *cols, shares)
    return outs[:2], outs[2:]


def bit_orders(bits):
    plain = list(range(1, bits))
    turned = plain[1::-1] + plain[2:]
    return plain, turned


def per_device(groups, tiles, features, occupancy, link_weights, basis_cols):
    lat, lon, words = features.shape
    share = words // tiles
    bits = tiles.bit_length() - 1
    orders = bit_orders(bits)
    tile = lax.axis_index("tile")

    def exchange(values, partner):
        pairs = []
        for g in range(groups):
            for t in range(tiles):
                to_g, to_t = partner(g, t)
                if not 0 <= to_t < tiles:
                    to_g, to_t = g ^ 1, t
                pairs.append((g * tiles + t, to_g % groups * tiles + to_t))
        return lax.ppermute(values, AXES, pairs)

    masked, proj, shares, row_a, row_b, *cols = project(
        occupancy, link_weights, features, basis_cols, 1 if groups <= 2 else 2
    )
    halo_row_b = exchange(row_b, lambda g, t: (g, t - 1 + 2 * (t % 2)))
    halo_cols = [exchange(cols[0], lambda g, t: (g + 1 - 2 * (g % 2), t))]
    if groups > 2:
        halo_cols.append(exchange(cols[1], lambda g, t: (g - 1 + 2 * (g % 2), t)))
    halo_row_a = exchange(row_a, lambda g, t: (g, t ^ 1))
    sends, keeps = partial_product(
        orders, share, masked, proj, (halo_row_a, halo_row_b), halo_cols, shares
    )
    parity = tile_parity()
    pick = functools.partial(lax.dynamic_index_in_dim, axis=0, keepdims=False)

    def partner_at(j):
        return lambda g, t: (g, t ^ (1 << orders[bin(t).count("1") & 1][j]) ^ 1)

    def reduced(held, send):
        got = exchange(send, lambda g, t: (g, t ^ 1))
        for j in range(bits - 2):
            mine = jnp.where(parity == 0, tile_bit(tile, orders[0][j]), tile_bit(tile, orders[1][j]))
            halves = (2, held.shape[0] // 2) + held.shape[1:]
            held, got = held.reshape(halves), got.reshape(halves)
            send = (pick(held, 1 - mine) + pick(got, 1 - mine).astype(F32)).astype(BF16)
            held = pick(held, mine) + pick(got, mine).astype(F32)
            got = exchange(send, partner_at(j))
        return held[0] + got[0].astype(F32)

    forward = exchange(reduced(keeps[0], sends[0]).astype(BF16), partner_at(bits - 2))
    total = reduced(keeps[1], sends[1]) + forward.astype(F32)
    step = 1
    while step < groups:
        send = total.astype(BF16)
        got = exchange(send, lambda g, t: (g ^ step, t))
        total = send.astype(F32) + got.astype(F32)
        step *= 2
    return total * (1.0 / math.sqrt(lat * lon * groups * tiles))


def solution(mesh):
    groups, tiles = mesh.shape["grp"], mesh.shape["tile"]
    placed = (P("tile", "grp", None), P("tile", "grp", None), P(None, "tile", "grp"), P())
    return jax.shard_map(
        functools.partial(per_device, groups, tiles),
        mesh=mesh, in_specs=placed, out_specs=P("tile", None), check_vma=False,
    )
```

```python
import functools
import math

import jax
import jax.numpy as jnp
from jax import lax
from jax.experimental import pallas as pl
from jax.experimental.pallas import tpu as pltpu
from jax.sharding import PartitionSpec as P

F32 = jnp.float32
BF16 = jnp.bfloat16
AXES = ("grp", "tile")
IN_HBM = pl.BlockSpec(memory_space=pltpu.HBM)
IN_VMEM = pl.BlockSpec(memory_space=pltpu.VMEM)
KERNEL_VMEM = 24 << 20
WORD_CHUNKS = (0.375, 0.375, 0.25)


def word_chunks(words):
    sizes = [int(words * part) for part in WORD_CHUNKS]
    return [(sum(sizes[:k]), size) for k, size in enumerate(sizes)]


def project_kernel(occ_hbm, links_hbm, feat_hbm, basis_hbm, masked, proj, shares, *rest):
    *edges, basis, total, links, occ, sems = rest
    row_a, row_b = edges[:2]
    lat, lon, words = masked.shape
    block = words // occ.shape[2]
    chunks = word_chunks(words)
    count = len(chunks)
    links_copy = pltpu.make_async_copy(links_hbm, links, sems.at[2 * count])
    occ_copy = pltpu.make_async_copy(occ_hbm, occ, sems.at[2 * count + 1])
    links_copy.start()
    occ_copy.start()
    copies = []
    for k, (start, size) in enumerate(chunks):
        part = pl.ds(start, size)
        basis_copy = pltpu.make_async_copy(basis_hbm.at[part], basis.at[part], sems.at[count + k])
        feat_copy = pltpu.make_async_copy(feat_hbm.at[:, :, part], masked.at[:, :, part], sems.at[k])
        basis_copy.start()
        feat_copy.start()
        copies.append((basis_copy, feat_copy))
    links_copy.wait()
    weights = links[...].astype(F32)
    weights = weights / jnp.maximum(jnp.sum(weights, axis=0), 1.0)
    for k in range(4):
        column = jnp.transpose(weights[k])
        for i in range(lat):
            shares[k, pl.ds(i * lon, lon), :] = jnp.broadcast_to(column[:, i:i + 1], (lon, shares.shape[2]))
    occ_copy.wait()
    for k, (start, size) in enumerate(chunks):
        copies[k][0].wait()
        copies[k][1].wait()
        for i in range(lat // 2):
            for b in range(start // block, (start + size) // block):
                gate = occ[i, 0, b].astype(F32).astype(BF16)
                spot = (pl.ds(2 * i, 2), slice(None), pl.ds(b * block, block))
                masked[spot] = masked[spot] * gate
        part = pl.ds(start, size)
        term = jnp.dot(
            masked[:, :, part].reshape(lat * lon, size), basis[part, :], preferred_element_type=F32
        )
        if k:
            term = total[...] + term
        if k < count - 1:
            total[...] = term
    rounded = term.astype(BF16)
    proj[...] = rounded.reshape(proj.shape)
    north, south = rounded[:lon], rounded[-lon:]
    even = lax.rem(lax.axis_index("tile"), 2) == 0
    row_a[...] = jnp.where(even, south, north)
    row_b[...] = jnp.where(even, north, south)
    grid = term.reshape(lat, lon, -1)
    west, east = grid[:, 0, :], grid[:, lon - 1, :]
    even = lax.rem(lax.axis_index("grp"), 2) == 0
    edges[2][...] = jnp.where(even, east, west).astype(BF16)
    if len(edges) > 3:
        edges[3][...] = jnp.where(even, west, east).astype(BF16)


def project(occupancy, link_weights, features, basis_cols, columns):
    lat, lon, words = features.shape
    rank = basis_cols.shape[1]
    operands = [
        pltpu.with_memory_space_constraint(v, pltpu.HBM)
        for v in (occupancy, link_weights, features, basis_cols)
    ]
    return pl.pallas_call(
        project_kernel,
        out_shape=(
            pltpu.VMEM((lat, lon, words), BF16),
            pltpu.VMEM((lat, lon, rank), BF16),
            pltpu.VMEM((4, lat * lon, min(rank, 128)), F32),
            pltpu.VMEM((lon, rank), BF16),
            pltpu.VMEM((lon, rank), BF16),
        ) + (pltpu.VMEM((lat, rank), BF16),) * columns,
        in_specs=[IN_HBM] * 4,
        out_specs=(IN_VMEM,) * (5 + columns),
        scratch_shapes=[
            pltpu.VMEM(basis_cols.shape, BF16),
            pltpu.VMEM((lat * lon, rank), F32),
            pltpu.VMEM(link_weights.shape, jnp.int32),
            pltpu.SMEM(occupancy.shape, jnp.int32),
            pltpu.SemaphoreType.DMA((2 * len(word_chunks(words)) + 2,)),
        ],
        compiler_params=pltpu.CompilerParams(vmem_limit_bytes=KERNEL_VMEM),
        cost_estimate=pl.CostEstimate(
            flops=2 * lat * lon * words * rank, bytes_accessed=2 * lat * lon * words, transcendentals=0
        ),
    )(*operands)


def smooth_rows(proj, north, south, west, east, shares, smooth):
    lat, lon, rank = proj.shape
    wide = rank // shares.shape[2]
    place = lax.broadcasted_iota(jnp.int32, (lon, rank), 0)
    for i in range(lat):
        row = proj[i].astype(F32)
        above = proj[i - 1].astype(F32) if i else north
        below = proj[i + 1].astype(F32) if i < lat - 1 else south
        left = jnp.where(place == 0, west[i:i + 1, :], pltpu.roll(row, 1, 0))
        right = jnp.where(place == lon - 1, east[i:i + 1, :], pltpu.roll(row, lon - 1, 0))
        link = [jnp.tile(shares[k, pl.ds(i * lon, lon), :], (1, wide)) for k in range(4)]
        value = link[0] * above + link[1] * below + link[2] * left + link[3] * right
        smooth[pl.ds(i * lon, lon), :] = value.astype(BF16)


def block_of(order, half, slot):
    steps = len(order)
    tile = sum(((slot >> (steps - 1 - j)) & 1) << bit for j, bit in enumerate(order))
    return tile + (half ^ (bin(tile).count("1") & 1))


def half_blocks(orders, sent, masked, values, outs):
    lat, lon, words = masked.shape
    places, share = outs[0].shape[:2]
    tile = lax.axis_index("tile")
    half = tile_parity() ^ sent
    own = jnp.where(half == 0, tile_bit(tile, orders[0][-1]), tile_bit(tile, orders[1][-1]))
    contract = (((0,), (0,)), ((), ()))
    if share % 128 == 0:
        count = max(1, 256 // share)
        for forward, out in ((1, outs[0]), (0, outs[1])):
            last = own ^ forward
            for place in range(0, places, count):
                parts = []
                for at in range(place, place + count):
                    block = [[block_of(order, h, 2 * at + low) for low in (0, 1)] for h, order in enumerate(orders)]
                    first = jnp.where(
                        half == 0,
                        jnp.where(last == 0, block[0][0], block[0][1]),
                        jnp.where(last == 0, block[1][0], block[1][1]),
                    ) * share
                    part = masked[:, :, pl.ds(pl.multiple_of(first, share), share)]
                    parts.append(part.reshape(lat * lon, share))
                part = jnp.concatenate(parts, axis=1) if count > 1 else parts[0]
                term = lax.dot_general(part, values, contract, preferred_element_type=F32)
                out[pl.ds(place, count)] = term.astype(out.dtype).reshape(count, share, -1)
        return
    slot_of = [
        {block_of(order, h, at) // 2: at for at in range(2 * places)} for h, order in enumerate(orders)
    ]
    step = 256
    for first in range(0, words, step):
        part = masked[:, :, pl.ds(first, step)].reshape(lat * lon, step)
        term = lax.dot_general(part, values, contract, preferred_element_type=F32)
        for at in range(0, step, 2 * share):
            pair = (first + at) // (2 * share)
            odd = bin(pair).count("1") & 1
            low, high = term[at:at + share], term[at + share:at + 2 * share]
            value = jnp.where(half == odd, low, high)
            slot = jnp.where(half == 0, slot_of[0][pair], slot_of[1][pair])
            for forward, out in ((1, outs[0]), (0, outs[1])):

                @pl.when(lax.rem(slot, 2) == own ^ forward)
                def _():
                    out[lax.div(slot, 2)] = value.astype(out.dtype)


def tile_bit(tile, bit):
    return lax.rem(lax.shift_right_logical(tile, bit), 2)


def tile_parity():
    tile = lax.axis_index("tile")
    parity = lax.rem(tile, 2)
    for bit in range(1, (lax.axis_size("tile") - 1).bit_length()):
        parity = parity ^ tile_bit(tile, bit)
    return parity


def ends(axis):
    place = lax.axis_index(axis)
    return place == 0, place == lax.axis_size(axis) - 1


def partial_kernel(orders, masked, proj, halo_row_a, halo_row_b, *rest):
    *rest, smooth = rest
    rest, sends, keeps = rest[:-4], rest[-4:-2], rest[-2:]
    *halo_cols, shares = rest
    row_a, row_b = halo_row_a[...].astype(F32), halo_row_b[...].astype(F32)
    odd = lax.rem(lax.axis_index("tile"), 2)
    first, last = ends("tile")
    north = jnp.where(first, 0.0, jnp.where(odd == 0, row_b, row_a))
    south = jnp.where(last, 0.0, jnp.where(odd == 0, row_a, row_b))
    col_a = halo_cols[0][...].astype(F32)
    col_b = halo_cols[1][...].astype(F32) if len(halo_cols) > 1 else jnp.zeros_like(col_a)
    even = lax.rem(lax.axis_index("grp"), 2) == 0
    first, last = ends("grp")
    west = jnp.where(first, 0.0, jnp.where(even, col_b, col_a))
    east = jnp.where(last, 0.0, jnp.where(even, col_a, col_b))
    smooth_rows(proj, north, south, west, east, shares, smooth)
    values = smooth[...]
    half_blocks(orders, 1, masked, values, sends)
    half_blocks(orders, 0, masked, values, keeps)


def partial_product(orders, share, masked, proj, rows, cols, shares):
    lat, lon, words = masked.shape
    rank = proj.shape[2]
    shape = (words // share // 4, share, rank)
    outs = pl.pallas_call(
        functools.partial(partial_kernel, orders),
        out_shape=(pltpu.VMEM(shape, BF16),) * 2 + (pltpu.VMEM(shape, F32),) * 2,
        in_specs=[IN_VMEM] * (5 + len(cols)),
        out_specs=(IN_VMEM,) * 4,
        scratch_shapes=[pltpu.VMEM((lat * lon, rank), BF16)],
        compiler_params=pltpu.CompilerParams(vmem_limit_bytes=KERNEL_VMEM),
        cost_estimate=pl.CostEstimate(
            flops=2 * lat * lon * words * rank, bytes_accessed=2 * lat * lon * words, transcendentals=0
        ),
    )(masked, proj, *rows, *cols, shares)
    return outs[:2], outs[2:]


def bit_orders(bits):
    base = list(range(1, bits))
    plain = base[:1] + base[:0:-1]
    turned = base[1::-1] + base[2:]
    return plain, turned


def per_device(groups, tiles, features, occupancy, link_weights, basis_cols):
    lat, lon, words = features.shape
    share = words // tiles
    bits = tiles.bit_length() - 1
    orders = bit_orders(bits)
    tile = lax.axis_index("tile")

    def exchange(values, partner):
        pairs = []
        for g in range(groups):
            for t in range(tiles):
                to_g, to_t = partner(g, t)
                if not 0 <= to_t < tiles:
                    to_g, to_t = g ^ 1, t
                pairs.append((g * tiles + t, to_g % groups * tiles + to_t))
        return lax.ppermute(values, AXES, pairs)

    masked, proj, shares, row_a, row_b, *cols = project(
        occupancy, link_weights, features, basis_cols, 1 if groups <= 2 else 2
    )
    halo_row_b = exchange(row_b, lambda g, t: (g, t - 1 + 2 * (t % 2)))
    halo_cols = [exchange(cols[0], lambda g, t: (g + 1 - 2 * (g % 2), t))]
    if groups > 2:
        halo_cols.append(exchange(cols[1], lambda g, t: (g - 1 + 2 * (g % 2), t)))
    halo_row_a = exchange(row_a, lambda g, t: (g, t ^ 1))
    sends, keeps = partial_product(
        orders, share, masked, proj, (halo_row_a, halo_row_b), halo_cols, shares
    )
    parity = tile_parity()
    pick = functools.partial(lax.dynamic_index_in_dim, axis=0, keepdims=False)

    def partner_at(j):
        return lambda g, t: (g, t ^ (1 << orders[bin(t).count("1") & 1][j]) ^ 1)

    def reduced(held, send):
        got = exchange(send, lambda g, t: (g, t ^ 1))
        for j in range(bits - 2):
            mine = jnp.where(parity == 0, tile_bit(tile, orders[0][j]), tile_bit(tile, orders[1][j]))
            halves = (2, held.shape[0] // 2) + held.shape[1:]
            held, got = held.reshape(halves), got.reshape(halves)
            send = (pick(held, 1 - mine) + pick(got, 1 - mine).astype(F32)).astype(BF16)
            held = pick(held, mine) + pick(got, mine).astype(F32)
            got = exchange(send, partner_at(j))
        return held[0] + got[0].astype(F32)

    onward = reduced(keeps[0], sends[0]).astype(BF16)
    partner = partner_at(bits - 2)
    forward = exchange(onward, partner)
    if groups == 2:
        across = exchange(onward, lambda g, t: (g ^ 1, partner(g, t)[1]))
        own = reduced(keeps[1], sends[1]).astype(BF16)
        other = exchange(own, lambda g, t: (g ^ 1, t))
        total = (own.astype(F32) + other.astype(F32)) + (forward.astype(F32) + across.astype(F32))
    else:
        total = reduced(keeps[1], sends[1]) + forward.astype(F32)
        step = 1
        while step < groups:
            send = total.astype(BF16)
            got = exchange(send, lambda g, t: (g ^ step, t))
            total = send.astype(F32) + got.astype(F32)
            step *= 2
    return total * (1.0 / math.sqrt(lat * lon * groups * tiles))


def solution(mesh):
    groups, tiles = mesh.shape["grp"], mesh.shape["tile"]
    placed = (P("tile", "grp", None), P("tile", "grp", None), P(None, "tile", "grp"), P())
    return jax.shard_map(
        functools.partial(per_device, groups, tiles),
        mesh=mesh, in_specs=placed, out_specs=P("tile", None), check_vma=False,
    )
```

```python
import functools
import math

import jax
import jax.numpy as jnp
from jax import lax
from jax.experimental import pallas as pl
from jax.experimental.pallas import tpu as pltpu
from jax.sharding import PartitionSpec as P

F32 = jnp.float32
BF16 = jnp.bfloat16
AXES = ("grp", "tile")
IN_HBM = pl.BlockSpec(memory_space=pltpu.HBM)
IN_VMEM = pl.BlockSpec(memory_space=pltpu.VMEM)
KERNEL_VMEM = 24 << 20
WORD_CHUNKS = (0.375, 0.375, 0.25)


def word_chunks(words):
    sizes = [int(words * part) for part in WORD_CHUNKS]
    return [(sum(sizes[:k]), size) for k, size in enumerate(sizes)]


def project_kernel(occ_hbm, links_hbm, feat_hbm, basis_hbm, masked, proj, shares, *rest):
    *edges, basis, total, links, occ, sems = rest
    row_a, row_b = edges[:2]
    lat, lon, words = masked.shape
    block = words // occ.shape[2]
    chunks = word_chunks(words)
    count = len(chunks)
    links_copy = pltpu.make_async_copy(links_hbm, links, sems.at[2 * count])
    occ_copy = pltpu.make_async_copy(occ_hbm, occ, sems.at[2 * count + 1])
    links_copy.start()
    occ_copy.start()
    copies = []
    for k, (start, size) in enumerate(chunks):
        part = pl.ds(start, size)
        basis_copy = pltpu.make_async_copy(basis_hbm.at[part], basis.at[part], sems.at[count + k])
        feat_copy = pltpu.make_async_copy(feat_hbm.at[:, :, part], masked.at[:, :, part], sems.at[k])
        basis_copy.start()
        feat_copy.start()
        copies.append((basis_copy, feat_copy))
    links_copy.wait()
    weights = links[...].astype(F32)
    weights = weights / jnp.maximum(jnp.sum(weights, axis=0), 1.0)
    for k in range(4):
        column = jnp.transpose(weights[k])
        for i in range(lat):
            shares[k, pl.ds(i * lon, lon), :] = jnp.broadcast_to(column[:, i:i + 1], (lon, shares.shape[2]))
    occ_copy.wait()
    for k, (start, size) in enumerate(chunks):
        copies[k][0].wait()
        copies[k][1].wait()
        for i in range(lat // 2):
            for b in range(start // block, (start + size) // block):
                gate = occ[i, 0, b].astype(F32).astype(BF16)
                spot = (pl.ds(2 * i, 2), slice(None), pl.ds(b * block, block))
                masked[spot] = masked[spot] * gate
        part = pl.ds(start, size)
        term = jnp.dot(
            masked[:, :, part].reshape(lat * lon, size), basis[part, :], preferred_element_type=F32
        )
        if k:
            term = total[...] + term
        if k < count - 1:
            total[...] = term
    rounded = term.astype(BF16)
    proj[...] = rounded.reshape(proj.shape)
    north, south = rounded[:lon], rounded[-lon:]
    even = lax.rem(lax.axis_index("tile"), 2) == 0
    row_a[...] = jnp.where(even, south, north)
    row_b[...] = jnp.where(even, north, south)
    grid = term.reshape(lat, lon, -1)
    west, east = grid[:, 0, :], grid[:, lon - 1, :]
    even = lax.rem(lax.axis_index("grp"), 2) == 0
    edges[2][...] = jnp.where(even, east, west).astype(BF16)
    if len(edges) > 3:
        edges[3][...] = jnp.where(even, west, east).astype(BF16)


def project(occupancy, link_weights, features, basis_cols, columns):
    lat, lon, words = features.shape
    rank = basis_cols.shape[1]
    operands = [
        pltpu.with_memory_space_constraint(v, pltpu.HBM)
        for v in (occupancy, link_weights, features, basis_cols)
    ]
    return pl.pallas_call(
        project_kernel,
        out_shape=(
            pltpu.VMEM((lat, lon, words), BF16),
            pltpu.VMEM((lat, lon, rank), BF16),
            pltpu.VMEM((4, lat * lon, min(rank, 128)), F32),
            pltpu.VMEM((lon, rank), BF16),
            pltpu.VMEM((lon, rank), BF16),
        ) + (pltpu.VMEM((lat, rank), BF16),) * columns,
        in_specs=[IN_HBM] * 4,
        out_specs=(IN_VMEM,) * (5 + columns),
        scratch_shapes=[
            pltpu.VMEM(basis_cols.shape, BF16),
            pltpu.VMEM((lat * lon, rank), F32),
            pltpu.VMEM(link_weights.shape, jnp.int32),
            pltpu.SMEM(occupancy.shape, jnp.int32),
            pltpu.SemaphoreType.DMA((2 * len(word_chunks(words)) + 2,)),
        ],
        compiler_params=pltpu.CompilerParams(vmem_limit_bytes=KERNEL_VMEM),
        cost_estimate=pl.CostEstimate(
            flops=2 * lat * lon * words * rank, bytes_accessed=2 * lat * lon * words, transcendentals=0
        ),
    )(*operands)


def smooth_rows(proj, north, south, west, east, shares, smooth):
    lat, lon, rank = proj.shape
    wide = rank // shares.shape[2]
    place = lax.broadcasted_iota(jnp.int32, (lon, rank), 0)
    above, row = north, proj[0].astype(F32)
    for i in range(lat):
        below = proj[i + 1].astype(F32) if i < lat - 1 else south
        left = jnp.where(place == 0, west[i:i + 1, :], pltpu.roll(row, 1, 0))
        right = jnp.where(place == lon - 1, east[i:i + 1, :], pltpu.roll(row, lon - 1, 0))
        link = [jnp.tile(shares[k, pl.ds(i * lon, lon), :], (1, wide)) for k in range(4)]
        value = link[0] * above + link[1] * below + link[2] * left + link[3] * right
        smooth[pl.ds(i * lon, lon), :] = value.astype(BF16)
        above, row = row, below


def block_of(order, half, slot):
    steps = len(order)
    tile = sum(((slot >> (steps - 1 - j)) & 1) << bit for j, bit in enumerate(order))
    return tile + (half ^ (bin(tile).count("1") & 1))


def half_blocks(orders, sent, masked, values, outs):
    lat, lon, words = masked.shape
    places, share = outs[0].shape[:2]
    tile = lax.axis_index("tile")
    half = tile_parity() ^ sent
    own = jnp.where(half == 0, tile_bit(tile, orders[0][-1]), tile_bit(tile, orders[1][-1]))
    contract = (((0,), (0,)), ((), ()))
    if share % 128 == 0:
        count = min(places, max(1, 512 // share))
        for forward, out in ((1, outs[0]), (0, outs[1])):
            last = own ^ forward
            for place in range(0, places, count):
                parts = []
                for at in range(place, place + count):
                    block = [[block_of(order, h, 2 * at + low) for low in (0, 1)] for h, order in enumerate(orders)]
                    first = jnp.where(
                        half == 0,
                        jnp.where(last == 0, block[0][0], block[0][1]),
                        jnp.where(last == 0, block[1][0], block[1][1]),
                    ) * share
                    part = masked[:, :, pl.ds(pl.multiple_of(first, share), share)]
                    parts.append(part.reshape(lat * lon, share))
                part = jnp.concatenate(parts, axis=1) if count > 1 else parts[0]
                term = lax.dot_general(part, values, contract, preferred_element_type=F32)
                out[pl.ds(place, count)] = term.astype(out.dtype).reshape(count, share, -1)
        return
    slot_of = [
        {block_of(order, h, at) // 2: at for at in range(2 * places)} for h, order in enumerate(orders)
    ]
    step = 256
    for first in range(0, words, step):
        part = masked[:, :, pl.ds(first, step)].reshape(lat * lon, step)
        term = lax.dot_general(part, values, contract, preferred_element_type=F32)
        for at in range(0, step, 2 * share):
            pair = (first + at) // (2 * share)
            odd = bin(pair).count("1") & 1
            low, high = term[at:at + share], term[at + share:at + 2 * share]
            value = jnp.where(half == odd, low, high)
            slot = jnp.where(half == 0, slot_of[0][pair], slot_of[1][pair])
            for forward, out in ((1, outs[0]), (0, outs[1])):

                @pl.when(lax.rem(slot, 2) == own ^ forward)
                def _():
                    out[lax.div(slot, 2)] = value.astype(out.dtype)


def tile_bit(tile, bit):
    return lax.rem(lax.shift_right_logical(tile, bit), 2)


def tile_parity():
    tile = lax.axis_index("tile")
    parity = lax.rem(tile, 2)
    for bit in range(1, (lax.axis_size("tile") - 1).bit_length()):
        parity = parity ^ tile_bit(tile, bit)
    return parity


def ends(axis):
    place = lax.axis_index(axis)
    return place == 0, place == lax.axis_size(axis) - 1


def partial_kernel(orders, masked, proj, halo_row_a, halo_row_b, *rest):
    *rest, smooth = rest
    rest, sends, keeps = rest[:-4], rest[-4:-2], rest[-2:]
    *halo_cols, shares = rest
    row_a, row_b = halo_row_a[...].astype(F32), halo_row_b[...].astype(F32)
    odd = lax.rem(lax.axis_index("tile"), 2)
    first, last = ends("tile")
    north = jnp.where(first, 0.0, jnp.where(odd == 0, row_b, row_a))
    south = jnp.where(last, 0.0, jnp.where(odd == 0, row_a, row_b))
    col_a = halo_cols[0][...].astype(F32)
    col_b = halo_cols[1][...].astype(F32) if len(halo_cols) > 1 else jnp.zeros_like(col_a)
    even = lax.rem(lax.axis_index("grp"), 2) == 0
    first, last = ends("grp")
    west = jnp.where(first, 0.0, jnp.where(even, col_b, col_a))
    east = jnp.where(last, 0.0, jnp.where(even, col_a, col_b))
    smooth_rows(proj, north, south, west, east, shares, smooth)
    values = smooth[...]
    half_blocks(orders, 1, masked, values, sends)
    half_blocks(orders, 0, masked, values, keeps)


def partial_product(orders, share, masked, proj, rows, cols, shares):
    lat, lon, words = masked.shape
    rank = proj.shape[2]
    shape = (words // share // 4, share, rank)
    outs = pl.pallas_call(
        functools.partial(partial_kernel, orders),
        out_shape=(pltpu.VMEM(shape, BF16),) * 2 + (pltpu.VMEM(shape, F32),) * 2,
        in_specs=[IN_VMEM] * (5 + len(cols)),
        out_specs=(IN_VMEM,) * 4,
        scratch_shapes=[pltpu.VMEM((lat * lon, rank), BF16)],
        compiler_params=pltpu.CompilerParams(vmem_limit_bytes=KERNEL_VMEM),
        cost_estimate=pl.CostEstimate(
            flops=2 * lat * lon * words * rank, bytes_accessed=2 * lat * lon * words, transcendentals=0
        ),
    )(masked, proj, *rows, *cols, shares)
    return outs[:2], outs[2:]


def bit_orders(bits):
    base = list(range(1, bits))
    plain = base[:1] + base[:0:-1]
    turned = base[1::-1] + base[2:]
    return plain, turned


def per_device(groups, tiles, features, occupancy, link_weights, basis_cols):
    lat, lon, words = features.shape
    share = words // tiles
    bits = tiles.bit_length() - 1
    orders = bit_orders(bits)
    tile = lax.axis_index("tile")

    def exchange(values, partner):
        pairs = []
        for g in range(groups):
            for t in range(tiles):
                to_g, to_t = partner(g, t)
                if not 0 <= to_t < tiles:
                    to_g, to_t = g ^ 1, t
                pairs.append((g * tiles + t, to_g % groups * tiles + to_t))
        return lax.ppermute(values, AXES, pairs)

    masked, proj, shares, row_a, row_b, *cols = project(
        occupancy, link_weights, features, basis_cols, 1 if groups <= 2 else 2
    )
    halo_row_b = exchange(row_b, lambda g, t: (g, t - 1 + 2 * (t % 2)))
    halo_cols = [exchange(cols[0], lambda g, t: (g + 1 - 2 * (g % 2), t))]
    if groups > 2:
        halo_cols.append(exchange(cols[1], lambda g, t: (g - 1 + 2 * (g % 2), t)))
    halo_row_a = exchange(row_a, lambda g, t: (g, t ^ 1))
    sends, keeps = partial_product(
        orders, share, masked, proj, (halo_row_a, halo_row_b), halo_cols, shares
    )
    parity = tile_parity()
    pick = functools.partial(lax.dynamic_index_in_dim, axis=0, keepdims=False)

    def partner_at(j):
        return lambda g, t: (g, t ^ (1 << orders[bin(t).count("1") & 1][j]) ^ 1)

    def reduced(held, send):
        got = exchange(send, lambda g, t: (g, t ^ 1))
        for j in range(bits - 2):
            mine = jnp.where(parity == 0, tile_bit(tile, orders[0][j]), tile_bit(tile, orders[1][j]))
            halves = (2, held.shape[0] // 2) + held.shape[1:]
            held, got = held.reshape(halves), got.reshape(halves)
            send = (pick(held, 1 - mine) + pick(got, 1 - mine).astype(F32)).astype(BF16)
            held = pick(held, mine) + pick(got, mine).astype(F32)
            got = exchange(send, partner_at(j))
        return held[0] + got[0].astype(F32)

    onward = reduced(keeps[0], sends[0]).astype(BF16)
    partner = partner_at(bits - 2)
    forward = exchange(onward, partner)
    if groups == 2:
        across = exchange(onward, lambda g, t: (g ^ 1, partner(g, t)[1]))
        own = reduced(keeps[1], sends[1]).astype(BF16)
        other = exchange(own, lambda g, t: (g ^ 1, t))
        total = (own.astype(F32) + other.astype(F32)) + (forward.astype(F32) + across.astype(F32))
    else:
        total = reduced(keeps[1], sends[1]) + forward.astype(F32)
        step = 1
        while step < groups:
            send = total.astype(BF16)
            got = exchange(send, lambda g, t: (g ^ step, t))
            total = send.astype(F32) + got.astype(F32)
            step *= 2
    return total * (1.0 / math.sqrt(lat * lon * groups * tiles))


def solution(mesh):
    groups, tiles = mesh.shape["grp"], mesh.shape["tile"]
    placed = (P("tile", "grp", None), P("tile", "grp", None), P(None, "tile", "grp"), P())
    return jax.shard_map(
        functools.partial(per_device, groups, tiles),
        mesh=mesh, in_specs=placed, out_specs=P("tile", None), check_vma=False,
    )
```
